32 devices in a mesh: groups: 2 (over y), filt: 4 (over z), sp: 2 (over x), in: 2 (over core).
Axes of the slice: x: 2, y: 2, z: 4, core: 2. Of those that a mesh axis runs over, the one named last changes fastest.
Arguments:
- image: bfloat16 [16, 256, 1024], P(('groups', 'sp', 'filt'), None, 'in'), parts along dimension 0, may hold values from -6 to 6
- weight: bfloat16 [3, 3, 1024, 1024], P(None, None, 'filt'), may hold values from -0.0625 to 0.0625
- bias: float32 [1024], P('filt'), may hold values from -3 to 3
- cotangent: bfloat16 [16, 1024, 256], P(('groups', 'sp'), 'filt'), parts along dimension 0, may hold values from -0.029907227 to 0.029907227
Outputs:
- output: bfloat16 [16, 1024, 256], P(('groups', 'sp', 'filt'), None, 'in'), parts along dimension 0
- grad_weight: float32 [6, 3, 1024, 1024], P('groups', None, 'filt', 'in'), parts along dimension 0
- grad_bias: float32 [2048], P(('groups', 'filt')), parts along dimension 0
The draws below stay inside these ranges and needn't reach their ends.
There are 2 independent parts, one for each index of `groups`. The reference program is written for one: setup_inputs(seed, part) draws one part's arguments, and reference() takes and returns one part's arrays. A program takes and returns all parts, laid end to end along the dimension named above; an argument that names none is the same for every part. Nothing has to cross between parts.
All inputs are finite; a program needn't handle non-finite values.
Results may differ from the reference program's by a relative error of at most 0.0055.
Values may be sent and summed in bfloat16 or wider, within the bound.
A program may use at most 64 MiB of HBM per device.

```python
import jax
import jax.numpy as jnp

CH = 1024
ROWS_DEV = 1
COLS = 256
ROWS = 8
N_FILT = 4
N_SP = 2


def shard_levels(own_key, dims, cuts, least, largest):
    def one(axis_at, shards_of):
        draws = jax.random.uniform(jax.random.fold_in(jax.random.fold_in(own_key, 6), axis_at), (shards_of,), jnp.float32, least / len(cuts), largest / len(cuts))
        return jnp.repeat(jnp.exp(draws), dims[axis_at] // shards_of).reshape((-1,) + (1,) * (len(dims) - axis_at - 1))

    level = one(*cuts[0])
    for cut in cuts[1:]:
        level = level * one(*cut)
    return level


def noise(key, dims, deviation, most, cuts=(), dtype=jnp.bfloat16):
    array = deviation * jax.random.normal(key, dims, jnp.float32)
    if cuts:
        array = array * shard_levels(key, dims, cuts, -0.22, 0.18)
    return jnp.clip(array, -most, most).astype(dtype)


def setup_inputs(seed: int = 0, part: int = 0) -> dict:
    key_of = jax.random.split(jax.random.key(seed), 5)
    part_keys = jax.random.split(jax.random.fold_in(key_of[4], part), 5)
    image = noise(part_keys[0], (ROWS, COLS, CH), 1.0, 6.0, ((0, 8), (2, 2)))
    weight = noise(key_of[1], (3, 3, CH, CH), (9 * CH) ** -0.5, 0.0625, ((2, 4),))
    bias = noise(key_of[2], (CH,), 0.5, 3.0, ((0, 4),), jnp.float32)
    cotangent = noise(part_keys[3], (ROWS, CH, COLS), 0.005, 0.029907227, ((0, 2), (1, 4)))
    return {"image": image, "weight": weight, "bias": bias, "cotangent": cotangent}


def reference(image, weight, bias, cotangent):
    row_count = ROWS_DEV * N_FILT * N_SP
    col_count = COLS
    padded = jnp.pad(image, ((1, 1), (1, 1), (0, 0)))
    running = jnp.zeros((row_count * col_count, CH), jnp.float32)
    for row_tap in range(3):
        for col_tap in range(3):
            window = padded[row_tap:row_tap + row_count, col_tap:col_tap + col_count].reshape(-1, CH)
            running = running + jnp.dot(window, weight[row_tap, col_tap].T, preferred_element_type=jnp.float32)
    shifted = running + bias[None, :]
    sigmoid_v = jax.nn.sigmoid(shifted)
    output = (shifted * sigmoid_v).astype(jnp.bfloat16).reshape(row_count, col_count, CH).transpose(0, 2, 1)
    slope = sigmoid_v * (1.0 + shifted * (1.0 - sigmoid_v))
    cot_rows = cotangent.transpose(0, 2, 1).reshape(-1, CH)
    grad_out = (cot_rows.astype(jnp.float32) * slope).astype(jnp.bfloat16)
    pieces = []
    for row_tap in range(3):
        for col_tap in range(3):
            window = padded[row_tap:row_tap + row_count, col_tap:col_tap + col_count].reshape(-1, CH)
            pieces.append(jnp.dot(grad_out.T, window, preferred_element_type=jnp.float32))
    grad_weight = jnp.stack(pieces).reshape(3, 3, CH, CH)
    grad_bias = jnp.sum(grad_out.astype(jnp.float32), axis=0)
    return (output, grad_weight, grad_bias)
```

```python
import functools

import jax
import jax.numpy as jnp
from jax import lax
from jax.experimental import pallas as pl
from jax.experimental.pallas import tpu as pltpu
from jax.sharding import PartitionSpec as P

MESH = pl.DeviceIdType.MESH
NT = (((1,), (1,)), ((), ()))


def shift_cols(value, by):
    cols = value.shape[1]
    col = lax.broadcasted_iota(jnp.int32, value.shape, 1)
    if by < 0:
        return jnp.where(col == 0, 0.0, pltpu.roll(value, 1, 1))
    return jnp.where(col == cols - 1, 0.0, pltpu.roll(value, cols - 1, 1))


def kernel(
    n_f, n_s,
    image, weight, bias, cotangent,
    out, gw, gb,
    rows, w, cot, part, peer, grads, act, gw_acc,
    load_sem, row_send, row_recv, x_send, sum_send, sum_recv,
    g_send, g_recv, h_send, h_recv, out_send, out_recv, gw_sem,
):
    p, s, c = lax.axis_index("filt"), lax.axis_index("sp"), lax.axis_index("in")
    sibling = 1 - c
    cols, depth = rows.shape[1], rows.shape[2]
    o = w.shape[2]
    half_o, half_c = o // 2, cols // 2
    total = n_f * n_s
    first = s * n_f
    x_peers = [lax.rem(s + d, n_s) for d in range(1, n_s)]

    load_row = pltpu.make_async_copy(image.at[0], rows.at[1 + first + p], load_sem.at[0])
    load_w = pltpu.make_async_copy(
        weight.at[:, :, :, pl.ds(pl.multiple_of(c * depth, depth), depth)], w, load_sem.at[1]
    )
    load_cot = pltpu.make_async_copy(cotangent, cot, load_sem.at[2])
    load_row.start()
    load_w.start()
    load_cot.start()

    barrier = pltpu.get_barrier_semaphore()
    for d in range(1, n_f):
        pl.semaphore_signal(barrier, 1, device_id={"filt": lax.rem(p + d, n_f)}, device_id_type=MESH)
    for peer_s in x_peers:
        pl.semaphore_signal(barrier, 1, device_id={"sp": peer_s}, device_id_type=MESH)
    pl.semaphore_signal(barrier, 1, device_id={"in": sibling}, device_id_type=MESH)
    zero = jnp.zeros((cols, depth), rows.dtype)
    rows[0] = zero
    rows[total + 1] = zero
    pl.semaphore_wait(barrier, n_f - 1 + n_s - 1 + 1)

    def row_copy(q, way, where, send):
        slot = rows.at[1 + q]
        return pltpu.make_async_remote_copy(
            src_ref=slot, dst_ref=slot, send_sem=send, recv_sem=row_recv.at[q],
            device_id={way: where}, device_id_type=MESH,
        )

    def to_right(q):
        return row_copy(first + q, "filt", p + 1, row_send.at[0, q])

    def to_left(q):
        return row_copy(first + q, "filt", p - 1, row_send.at[1, q])

    def to_x(q, d):
        return row_copy(first + q, "sp", x_peers[d], x_send.at[d, q])

    def wait_row(q):
        row_copy(q, "filt", p, row_send.at[0, 0]).wait_recv()

    def pass_on(q, right, left):
        if right:
            @pl.when(p + 1 < n_f)
            def _():
                to_right(q).start()
        if left:
            @pl.when(p >= 1)
            def _():
                to_left(q).start()
        for d in range(n_s - 1):
            to_x(q, d).start()

    load_row.wait()
    pass_on(p, True, True)
    for t in range(1, n_f):
        @pl.when(p - t >= 0)
        def _():
            wait_row(first + p - t)
            pass_on(p - t, True, False)

        @pl.when(p + t < n_f)
        def _():
            wait_row(first + p + t)
            pass_on(p + t, False, True)

    load_w.wait()
    load_cot.wait()

    @pl.when(s > 0)
    def _():
        wait_row(first - 1)

    @pl.when(s + 1 < n_s)
    def _():
        wait_row(first + n_f)

    def sum_copy(r):
        return pltpu.make_async_remote_copy(
            src_ref=part.at[r], dst_ref=peer.at[r], send_sem=sum_send.at[r], recv_sem=sum_recv.at[r],
            device_id={"in": sibling}, device_id_type=MESH,
        )

    @pl.loop(0, n_f)
    def _(r):
        sums = jnp.zeros((3 * o, cols), jnp.float32)
        for a in range(3):
            sums = sums + lax.dot_general(
                w[a].reshape(3 * o, depth), rows[first + r + a], NT, preferred_element_type=jnp.float32
            )
        part[r] = shift_cols(sums[:o], -1) + sums[o:2 * o] + shift_cols(sums[2 * o:], 1)
        sum_copy(r).start()

    bias_all = jnp.broadcast_to(bias[...], (cols, o)).T

    def out_copy(r):
        return pltpu.make_async_remote_copy(
            src_ref=act.at[r, :, pl.ds(pl.multiple_of(c * half_c, half_c), half_c)],
            dst_ref=out.at[0, pl.ds(pl.multiple_of(p * o, o), o), :],
            send_sem=out_send.at[r], recv_sem=out_recv.at[p],
            device_id={"filt": r}, device_id_type=MESH,
        )

    own_out = pltpu.make_async_copy(
        act.at[p, :, pl.ds(pl.multiple_of(c * half_c, half_c), half_c)],
        out.at[0, pl.ds(pl.multiple_of(p * o, o), o), :],
        load_sem.at[0],
    )

    def lanes(q, count=1):
        return pl.ds(pl.multiple_of(q * cols, cols), count * cols)

    @pl.loop(0, n_f)
    def _(r):
        sum_copy(r).wait_recv()
        shifted = part[r] + peer[r] + bias_all
        sig = jax.nn.sigmoid(shifted)
        act[r] = (shifted * sig).astype(jnp.bfloat16)
        slope = sig * (1.0 + shifted * (1.0 - sig))
        grad = (cot[r].astype(jnp.float32) * slope).astype(jnp.bfloat16)
        grads[1, :, lanes(first + r)] = grad
        wide = grad.astype(jnp.float32)
        grads[0, :, lanes(first + r)] = shift_cols(wide, 1).astype(jnp.bfloat16)
        grads[2, :, lanes(first + r)] = shift_cols(wide, -1).astype(jnp.bfloat16)

        @pl.when(r == p)
        def _():
            own_out.start()

        @pl.when(r != p)
        def _():
            out_copy(r).start()

    def g_part(block, core):
        return grads.at[
            1, pl.ds(pl.multiple_of(core * half_o, half_o), half_o), lanes(block * n_f, n_f)
        ]

    def g_copy(d):
        return pltpu.make_async_remote_copy(
            src_ref=g_part(s, c), dst_ref=g_part(s, c), send_sem=g_send.at[d], recv_sem=g_recv.at[s],
            device_id={"sp": x_peers[d]}, device_id_type=MESH,
        )

    def g_wait(block, core, recv):
        pltpu.make_async_remote_copy(
            src_ref=g_part(block, core), dst_ref=g_part(block, core), send_sem=g_send.at[0], recv_sem=recv,
            device_id={"in": sibling}, device_id_type=MESH,
        ).wait_recv()

    def h_copy(d):
        block = x_peers[d]
        return pltpu.make_async_remote_copy(
            src_ref=g_part(block, c), dst_ref=g_part(block, c), send_sem=h_send.at[d], recv_sem=h_recv.at[block],
            device_id={"in": sibling}, device_id_type=MESH,
        )

    for d in range(n_s - 1):
        g_copy(d).start()

    def tap(a, b, block):
        window = rows[pl.ds(block * n_f + a, n_f)].reshape(n_f * cols, depth)
        return jnp.dot(
            grads[b, :, lanes(block * n_f, n_f)], window, preferred_element_type=jnp.float32
        )

    @pl.loop(0, 9)
    def _(k):
        gw_acc[k] = tap(k // 3, lax.rem(k, 3), s)

    for d in range(n_s - 1):
        g_wait(x_peers[d], c, g_recv.at[x_peers[d]])
        h_copy(d).start()

    for d in range(n_s - 1):
        for q in range(n_f):
            row = x_peers[d] * n_f + q

            @pl.when((row != first - 1) & (row != first + n_f))
            def _():
                wait_row(row)

    def gw_copy(k):
        return pltpu.make_async_copy(gw_acc.at[k], gw.at[k // 3, lax.rem(k, 3)], gw_sem.at[k])

    for d in range(n_s - 1):
        block = x_peers[d]
        g_wait(block, sibling, h_recv.at[block])
        h_copy(d).wait_send()

        @pl.loop(0, n_f)
        def _(r):
            wide = grads[1, :, lanes(block * n_f + r)].astype(jnp.float32)
            grads[0, :, lanes(block * n_f + r)] = shift_cols(wide, 1).astype(jnp.bfloat16)
            grads[2, :, lanes(block * n_f + r)] = shift_cols(wide, -1).astype(jnp.bfloat16)

        @pl.loop(0, 9)
        def _(k):
            gw_acc[k] += tap(k // 3, lax.rem(k, 3), block)
            if d == n_s - 2:
                gw_copy(k).start()

    gb[...] = lax.dot_general(
        jnp.ones((8, total * cols), jnp.bfloat16), grads[1], NT, preferred_element_type=jnp.float32
    )

    @pl.loop(0, n_f)
    def _(r):
        sum_copy(r).wait_send()

        @pl.when(r == p)
        def _():
            own_out.wait()

        @pl.when(r != p)
        def _():
            out_copy(r).wait_send()
            pltpu.make_async_remote_copy(
                src_ref=act.at[r, :, pl.ds(0, half_c)],
                dst_ref=out.at[0, pl.ds(pl.multiple_of(r * o, o), o), :],
                send_sem=out_send.at[r], recv_sem=out_recv.at[r],
                device_id={"filt": r}, device_id_type=MESH,
            ).wait_recv()

        for d in range(n_s - 1):
            to_x(r, d).wait_send()

        @pl.when((r <= p) & (p + 1 < n_f))
        def _():
            to_right(r).wait_send()

        @pl.when((r >= p) & (p >= 1))
        def _():
            to_left(r).wait_send()

    for d in range(n_s - 1):
        g_copy(d).wait_send()

    @pl.loop(0, 9)
    def _(k):
        gw_copy(k).wait()


def on_device(image, weight, bias, cotangent):
    n_f, n_s, n_in = (lax.axis_size(name) for name in ("filt", "sp", "in"))
    row_count, o, cols = cotangent.shape
    depth = image.shape[2]
    total = n_f * n_s
    any_space = pl.BlockSpec(memory_space=pl.ANY)
    vmem = pl.BlockSpec(memory_space=pltpu.VMEM)
    dma = pltpu.SemaphoreType.DMA
    output, grad_weight, grad_bias = pl.pallas_call(
        functools.partial(kernel, n_f, n_s),
        out_shape=(
            jax.ShapeDtypeStruct((1, n_f * o, cols // n_in), jnp.bfloat16),
            jax.ShapeDtypeStruct((3, 3, o, depth), jnp.float32),
            jax.ShapeDtypeStruct((8, o), jnp.float32),
        ),
        in_specs=[any_space, any_space, vmem, any_space],
        out_specs=(any_space, any_space, vmem),
        scratch_shapes=[
            pltpu.VMEM((total + 2, cols, depth), jnp.bfloat16),
            pltpu.VMEM((3, 3, o, depth), jnp.bfloat16),
            pltpu.VMEM((n_f, o, cols), jnp.bfloat16),
            pltpu.VMEM((n_f, o, cols), jnp.float32),
            pltpu.VMEM((n_f, o, cols), jnp.float32),
            pltpu.VMEM((3, o, total * cols), jnp.bfloat16),
            pltpu.VMEM((n_f, o, cols), jnp.bfloat16),
            pltpu.VMEM((9, o, depth), jnp.float32),
            dma((3,)),
            dma((2, n_f)),
            dma((total,)),
            dma((n_s - 1, n_f)),
            dma((n_f,)),
            dma((n_f,)),
            dma((n_s - 1,)),
            dma((n_s,)),
            dma((n_s - 1,)),
            dma((n_s,)),
            dma((n_f,)),
            dma((n_f,)),
            dma((9,)),
        ],
        compiler_params=pltpu.CompilerParams(
            collective_id=0, has_side_effects=True, vmem_limit_bytes=60 * 1024 * 1024
        ),
    )(image, weight, bias.reshape(1, o), cotangent)
    return (output, grad_weight, grad_bias[0])


def solution(mesh):
    placed = (
        P(("groups", "sp", "filt"), None, "in"),
        P(None, None, "filt", None),
        P("filt"),
        P(("groups", "sp"), "filt", None),
    )
    return jax.shard_map(
        on_device,
        mesh=mesh,
        in_specs=placed,
        out_specs=(
            P(("groups", "sp", "filt"), None, "in"),
            P("groups", None, "filt", "in"),
            P(("groups", "filt")),
        ),
        check_vma=False,
    )
```

```python
import functools

import jax
import jax.numpy as jnp
from jax import lax
from jax.experimental import pallas as pl
from jax.experimental.pallas import tpu as pltpu
from jax.sharding import PartitionSpec as P

MESH = pl.DeviceIdType.MESH
NT = (((1,), (1,)), ((), ()))


def shift_cols(value, by):
    cols = value.shape[1]
    col = lax.broadcasted_iota(jnp.int32, value.shape, 1)
    if by < 0:
        return jnp.where(col == 0, 0.0, pltpu.roll(value, 1, 1))
    return jnp.where(col == cols - 1, 0.0, pltpu.roll(value, cols - 1, 1))


def lanes(q, cols, count=1):
    return pl.ds(pl.multiple_of(q * cols, cols), count * cols)


def store_shifts(grads, place, grad):
    wide = grad.astype(jnp.float32)
    grads[0, :, place] = shift_cols(wide, 1).astype(jnp.bfloat16)
    grads[2, :, place] = shift_cols(wide, -1).astype(jnp.bfloat16)


def block_tap(rows, grads, a, b, block, n_f):
    cols, depth = rows.shape[1], rows.shape[2]
    window = rows[pl.ds(block * n_f + a, n_f)].reshape(n_f * cols, depth)
    return jnp.dot(
        grads[b, :, lanes(block * n_f, cols, n_f)], window, preferred_element_type=jnp.float32
    )


def gather_kernel(
    n_f, n_s,
    image, weight, bias_in, cotangent,
    rows, grads, gw_own, out,
    w, bias, cot, part, peer, act,
    load_sem, row_send, row_recv, x_send, sum_send, sum_recv,
    g_send, g_recv, out_send, out_recv,
):
    p, s, c = lax.axis_index("filt"), lax.axis_index("sp"), lax.axis_index("in")
    sibling = 1 - c
    cols, depth = rows.shape[1], rows.shape[2]
    o = w.shape[2]
    half_c = out.shape[1]
    total = n_f * n_s
    first = s * n_f
    last = n_f - 1
    x_peers = [lax.rem(s + d, n_s) for d in range(1, n_s)]

    load_row = pltpu.make_async_copy(image.at[0], rows.at[1 + first + p], load_sem.at[0])
    load_w = pltpu.make_async_copy(
        weight.at[:, :, :, pl.ds(pl.multiple_of(c * depth, depth), depth)], w, load_sem.at[1]
    )
    load_cot = pltpu.make_async_copy(cotangent, cot, load_sem.at[2])
    load_bias = pltpu.make_async_copy(bias_in, bias, load_sem.at[3])
    load_row.start()
    load_w.start()
    load_cot.start()
    load_bias.start()

    barrier = pltpu.get_barrier_semaphore()
    for d in range(1, n_f):
        pl.semaphore_signal(barrier, 1, device_id={"filt": lax.rem(p + d, n_f)}, device_id_type=MESH)
    for peer_s in x_peers:
        pl.semaphore_signal(barrier, 1, device_id={"sp": peer_s}, device_id_type=MESH)
    pl.semaphore_signal(barrier, 1, device_id={"in": sibling}, device_id_type=MESH)
    pl.semaphore_wait(barrier, n_f - 1 + n_s - 1 + 1)

    def row_copy(q, way, where, send):
        slot = rows.at[1 + q]
        return pltpu.make_async_remote_copy(
            src_ref=slot, dst_ref=slot, send_sem=send, recv_sem=row_recv.at[q],
            device_id={way: where}, device_id_type=MESH,
        )

    def to_right(q):
        return row_copy(q, "filt", p + 1, row_send.at[0, q])

    def to_left(q):
        return row_copy(q, "filt", p - 1, row_send.at[1, q])

    def to_x(q, d):
        return row_copy(first + q, "sp", x_peers[d], x_send.at[d, q])

    def wait_row(q):
        row_copy(q, "filt", p, row_send.at[0, 0]).wait_recv()

    def crosses(q):
        return ((q > 0) & (q < last)) | (q == p)

    def pass_on(q, right, left):
        if right:
            @pl.when(p < last)
            def _():
                to_right(first + q).start()
        if left:
            @pl.when(p > 0)
            def _():
                to_left(first + q).start()

        @pl.when(crosses(q))
        def _():
            for d in range(n_s - 1):
                to_x(q, d).start()

    load_row.wait()
    pass_on(p, True, True)

    zero = jnp.zeros((cols, depth), rows.dtype)
    rows[0] = zero
    rows[total + 1] = zero

    @pl.loop(0, n_f + 2)
    def _(r):
        part[r] = jnp.zeros((o, cols), jnp.float32)

    load_w.wait()

    def add_tap(q, a, r):
        sums = lax.dot_general(
            w[a].reshape(3 * o, depth), rows[1 + q], NT, preferred_element_type=jnp.float32
        )
        part[r + 1] += shift_cols(sums[:o], -1) + sums[o:2 * o] + shift_cols(sums[2 * o:], 1)

    def add_row(q):
        for a in range(3):
            add_tap(first + q, a, q - a + 1)

    def sum_copy(r):
        return pltpu.make_async_remote_copy(
            src_ref=part.at[r + 1], dst_ref=peer.at[r], send_sem=sum_send.at[r], recv_sem=sum_recv.at[r],
            device_id={"in": sibling}, device_id_type=MESH,
        )

    def out_copy(r):
        return pltpu.make_async_remote_copy(
            src_ref=act.at[r, :, pl.ds(pl.multiple_of(c * half_c, half_c), half_c)],
            dst_ref=out.at[pl.ds(pl.multiple_of(p * o, o), o), :],
            send_sem=out_send.at[r], recv_sem=out_recv.at[p],
            device_id={"filt": r}, device_id_type=MESH,
        )

    own_out = pltpu.make_async_copy(
        act.at[p, :, pl.ds(pl.multiple_of(c * half_c, half_c), half_c)],
        out.at[pl.ds(pl.multiple_of(p * o, o), o), :],
        load_sem.at[0],
    )

    def g_copy(q, d):
        place = grads.at[1, :, lanes(q, cols)]
        return pltpu.make_async_remote_copy(
            src_ref=place, dst_ref=place, send_sem=g_send.at[d, q], recv_sem=g_recv.at[q],
            device_id={"sp": x_peers[d]}, device_id_type=MESH,
        )

    def done_at(r):
        low = jnp.where(s == 0, jnp.maximum(p, 1), jnp.maximum(p, n_f - p))
        high = jnp.where(
            s == n_s - 1, jnp.maximum(last - p, 1), jnp.maximum(last - p, p + 1)
        )
        return jnp.where(r == 0, low, jnp.where(r == last, high, jnp.abs(r - p) + 1))

    def finish(r):
        sum_copy(r).wait_recv()
        bias_all = jnp.broadcast_to(bias[...], (cols, o)).T
        shifted = part[r + 1] + peer[r] + bias_all
        sig = jax.nn.sigmoid(shifted)
        slope = sig * (1.0 + shifted * (1.0 - sig))
        grad = (cot[r].astype(jnp.float32) * slope).astype(jnp.bfloat16)
        place = lanes(first + r, cols)
        grads[1, :, place] = grad
        act[r] = (shifted * sig).astype(jnp.bfloat16)
        for d in range(n_s - 1):
            g_copy(first + r, d).start()

        @pl.when(r == p)
        def _():
            own_out.start()

        @pl.when(r != p)
        def _():
            out_copy(r).start()

        store_shifts(grads, place, grad)

    add_row(p)
    load_cot.wait()
    load_bias.wait()

    @pl.loop(1, n_f + 2)
    def _(t):
        @pl.when(p - t >= 0)
        def _():
            wait_row(first + p - t)
            pass_on(p - t, True, False)

        @pl.when(p + t < n_f)
        def _():
            wait_row(first + p + t)
            pass_on(p + t, False, True)

        @pl.when(t == p + 1)
        def _():
            for block in x_peers:
                wait_row(block * n_f)

                @pl.when(p < last)
                def _():
                    to_right(block * n_f).start()

        @pl.when(t == n_f - p)
        def _():
            for block in x_peers:
                wait_row(block * n_f + last)

                @pl.when(p > 0)
                def _():
                    to_left(block * n_f + last).start()

        @pl.when(p - t >= 0)
        def _():
            add_row(p - t)

        @pl.when(p + t < n_f)
        def _():
            add_row(p + t)

        @pl.when((t == p + 1) & (s < n_s - 1))
        def _():
            add_tap(first + n_f, 2, last)

        @pl.when((t == n_f - p) & (s > 0))
        def _():
            add_tap(first - 1, 0, 0)

        @pl.loop(0, n_f)
        def _(r):
            @pl.when(done_at(r) == t)
            def _():
                sum_copy(r).start()

        @pl.loop(0, n_f)
        def _(r):
            @pl.when(done_at(r) == t - 1)
            def _():
                finish(r)

    @pl.loop(0, 9)
    def _(k):
        gw_own[k] = block_tap(rows, grads, k // 3, lax.rem(k, 3), s, n_f)

    for block in x_peers:
        @pl.loop(1, last)
        def _(q):
            wait_row(block * n_f + q)

        @pl.loop(0, n_f)
        def _(q):
            g_copy(block * n_f + q, 0).wait_recv()
            place = lanes(block * n_f + q, cols)
            store_shifts(grads, place, grads[1, :, place])

    @pl.loop(0, n_f)
    def _(r):
        sum_copy(r).wait_send()

        @pl.when(r == p)
        def _():
            own_out.wait()

        @pl.when(r != p)
        def _():
            out_copy(r).wait_send()
            pltpu.make_async_remote_copy(
                src_ref=act.at[r, :, pl.ds(0, half_c)],
                dst_ref=out.at[pl.ds(pl.multiple_of(r * o, o), o), :],
                send_sem=out_send.at[r], recv_sem=out_recv.at[r],
                device_id={"filt": r}, device_id_type=MESH,
            ).wait_recv()

        for d in range(n_s - 1):
            g_copy(first + r, d).wait_send()

            @pl.when(crosses(r))
            def _():
                to_x(r, d).wait_send()

        @pl.when((r <= p) & (p < last))
        def _():
            to_right(first + r).wait_send()

        @pl.when((r >= p) & (p > 0))
        def _():
            to_left(first + r).wait_send()

    for block in x_peers:
        @pl.when(p < last)
        def _():
            to_right(block * n_f).wait_send()

        @pl.when(p > 0)
        def _():
            to_left(block * n_f + last).wait_send()


def finish_kernel(n_f, n_s, rows, grads, gw_own, out_in, gw, gb, out, total, sem, out_sem):
    s = lax.axis_index("sp")
    out_copy = pltpu.make_async_copy(out_in, out.at[0], out_sem)
    out_copy.start()

    def gw_copy(k):
        return pltpu.make_async_copy(total.at[k], gw.at[k // 3, lax.rem(k, 3)], sem.at[k])

    @pl.loop(0, 9)
    def _(k):
        value = gw_own[k]
        for d in range(1, n_s):
            value = value + block_tap(rows, grads, k // 3, lax.rem(k, 3), lax.rem(s + d, n_s), n_f)
        total[k] = value
        gw_copy(k).start()

    gb[...] = lax.dot_general(
        jnp.ones((8, grads.shape[2]), jnp.bfloat16), grads[1], NT, preferred_element_type=jnp.float32
    )[:1]

    @pl.loop(0, 9)
    def _(k):
        gw_copy(k).wait()

    out_copy.wait()


def on_device(image, weight, bias, cotangent):
    n_f, n_s, n_in = (lax.axis_size(name) for name in ("filt", "sp", "in"))
    row_count, o, cols = cotangent.shape
    depth = image.shape[2]
    total = n_f * n_s
    any_space = pl.BlockSpec(memory_space=pl.ANY)
    vmem = pl.BlockSpec(memory_space=pltpu.VMEM)
    hbm = pl.BlockSpec(memory_space=pltpu.HBM)
    dma = pltpu.SemaphoreType.DMA
    between = pl.pallas_call(
        functools.partial(gather_kernel, n_f, n_s),
        out_shape=(
            pltpu.VMEM((total + 2, cols, depth), jnp.bfloat16),
            pltpu.VMEM((3, o, total * cols), jnp.bfloat16),
            pltpu.VMEM((9, o, depth), jnp.float32),
            pltpu.VMEM((n_f * o, cols // n_in), jnp.bfloat16),
        ),
        in_specs=[hbm, hbm, hbm, hbm],
        out_specs=(vmem,) * 4,
        scratch_shapes=[
            pltpu.VMEM((3, 3, o, depth), jnp.bfloat16),
            pltpu.VMEM((1, o), jnp.float32),
            pltpu.VMEM((n_f, o, cols), jnp.bfloat16),
            pltpu.VMEM((n_f + 2, o, cols), jnp.float32),
            pltpu.VMEM((n_f, o, cols), jnp.float32),
            pltpu.VMEM((n_f, o, cols), jnp.bfloat16),
            dma((4,)),
            dma((2, total)),
            dma((total,)),
            dma((n_s - 1, n_f)),
            dma((n_f,)),
            dma((n_f,)),
            dma((n_s - 1, total)),
            dma((total,)),
            dma((n_f,)),
            dma((n_f,)),
        ],
        compiler_params=pltpu.CompilerParams(
            collective_id=0, has_side_effects=True, vmem_limit_bytes=24 * 1024 * 1024
        ),
        name="gather",
    )(*(
        pltpu.with_memory_space_constraint(x, pltpu.HBM)
        for x in (image, weight, bias.reshape(1, o), cotangent)
    ))
    grad_weight, grad_bias, output = pl.pallas_call(
        functools.partial(finish_kernel, n_f, n_s),
        out_shape=(
            jax.ShapeDtypeStruct((3, 3, o, depth), jnp.float32),
            jax.ShapeDtypeStruct((1, o), jnp.float32),
            jax.ShapeDtypeStruct((1, n_f * o, cols // n_in), jnp.bfloat16),
        ),
        in_specs=[vmem] * 4,
        out_specs=(any_space, vmem, any_space),
        scratch_shapes=[
            pltpu.VMEM((9, o, depth), jnp.float32),
            dma((9,)),
            dma(()),
        ],
        compiler_params=pltpu.CompilerParams(vmem_limit_bytes=20 * 1024 * 1024),
        name="finish",
    )(*between)
    return (output, grad_weight, grad_bias.reshape(o))


def solution(mesh):
    placed = (
        P(("groups", "sp", "filt"), None, "in"),
        P(None, None, "filt", None),
        P("filt"),
        P(("groups", "sp"), "filt", None),
    )
    return jax.shard_map(
        on_device,
        mesh=mesh,
        in_specs=placed,
        out_specs=(
            P(("groups", "sp", "filt"), None, "in"),
            P("groups", None, "filt", "in"),
            P(("groups", "filt")),
        ),
        check_vma=False,
    )
```

```python
import functools

import jax
import jax.numpy as jnp
from jax import lax
from jax.experimental import pallas as pl
from jax.experimental.pallas import tpu as pltpu
from jax.sharding import PartitionSpec as P

MESH = pl.DeviceIdType.MESH
NT = (((1,), (1,)), ((), ()))


def shift_cols(value, by):
    cols = value.shape[1]
    col = lax.broadcasted_iota(jnp.int32, value.shape, 1)
    if by < 0:
        return jnp.where(col == 0, 0.0, pltpu.roll(value, 1, 1))
    return jnp.where(col == cols - 1, 0.0, pltpu.roll(value, cols - 1, 1))


def lanes(q, cols, count=1):
    return pl.ds(pl.multiple_of(q * cols, cols), count * cols)


def store_shifts(grads, place, grad):
    wide = grad.astype(jnp.float32)
    grads[0, :, place] = shift_cols(wide, 1).astype(jnp.bfloat16)
    grads[2, :, place] = shift_cols(wide, -1).astype(jnp.bfloat16)


def rows_tap(rows, grads, a, b, start, count):
    cols, depth = rows.shape[1], rows.shape[2]
    window = rows[pl.ds(start + a, count)].reshape(count * cols, depth)
    return jnp.dot(
        grads[b, :, lanes(start, cols, count)], window, preferred_element_type=jnp.float32
    )


def late_row(block, n_f):
    return block * n_f + jnp.where(block > 0, 0, n_f - 1)


def early_row(block, n_f):
    return block * n_f + jnp.where(block > 0, 1, 0)


def gather_kernel(
    n_f, n_s,
    image, weight, bias_in, cotangent,
    rows, grads, gw_own, out,
    w, bias, cot, part, peer, act,
    load_sem, row_send, row_recv, x_send, sum_send, sum_recv,
    g_send, g_recv, out_send, out_recv,
):
    p, s, c = lax.axis_index("filt"), lax.axis_index("sp"), lax.axis_index("in")
    sibling = 1 - c
    cols, depth = rows.shape[1], rows.shape[2]
    o = w.shape[2]
    half_c = out.shape[1]
    total = n_f * n_s
    first = s * n_f
    last = n_f - 1
    x_peers = [lax.rem(s + d, n_s) for d in range(1, n_s)]

    load_row = pltpu.make_async_copy(image.at[0], rows.at[1 + first + p], load_sem.at[0])
    load_w = pltpu.make_async_copy(
        weight.at[:, :, :, pl.ds(pl.multiple_of(c * depth, depth), depth)], w, load_sem.at[1]
    )
    load_cot = pltpu.make_async_copy(cotangent, cot, load_sem.at[2])
    load_bias = pltpu.make_async_copy(bias_in, bias, load_sem.at[3])
    load_row.start()
    load_w.start()
    load_cot.start()
    load_bias.start()

    barrier = pltpu.get_barrier_semaphore()
    for d in range(1, n_f):
        pl.semaphore_signal(barrier, 1, device_id={"filt": lax.rem(p + d, n_f)}, device_id_type=MESH)
    for peer_s in x_peers:
        pl.semaphore_signal(barrier, 1, device_id={"sp": peer_s}, device_id_type=MESH)
    pl.semaphore_signal(barrier, 1, device_id={"in": sibling}, device_id_type=MESH)
    pl.semaphore_wait(barrier, n_f - 1 + n_s - 1 + 1)

    piece = cols // 2

    def row_copy(q, h, way, where, send):
        slot = rows.at[1 + q, pl.ds(h * piece, piece)]
        return pltpu.make_async_remote_copy(
            src_ref=slot, dst_ref=slot, send_sem=send, recv_sem=row_recv.at[q, h],
            device_id={way: where}, device_id_type=MESH,
        )

    def to_right(q, h):
        return row_copy(q, h, "filt", p + 1, row_send.at[0, q, h])

    def to_left(q, h):
        return row_copy(q, h, "filt", p - 1, row_send.at[1, q, h])

    def to_x(q, h, d):
        return row_copy(first + q, h, "sp", x_peers[d], x_send.at[d, q, h])

    def wait_row(q, h):
        row_copy(q, h, "filt", p, row_send.at[0, 0, 0]).wait_recv()

    def crosses(q):
        return ((q > 0) & (q < last)) | (q == p)

    def pass_on(q, h, right, left):
        if right:
            @pl.when(p < last)
            def _():
                to_right(first + q, h).start()
        if left:
            @pl.when(p > 0)
            def _():
                to_left(first + q, h).start()

        @pl.when(crosses(q))
        def _():
            for d in range(n_s - 1):
                to_x(q, h, d).start()

    load_row.wait()
    for h in range(2):
        pass_on(p, h, True, True)

    zero = jnp.zeros((cols, depth), rows.dtype)
    rows[0] = zero
    rows[total + 1] = zero

    @pl.loop(0, n_f + 2)
    def _(r):
        part[r] = jnp.zeros((o, cols), jnp.float32)

    load_w.wait()

    def add_tap(q, a, r):
        sums = lax.dot_general(
            w[a].reshape(3 * o, depth), rows[1 + q], NT, preferred_element_type=jnp.float32
        )
        part[r + 1] += shift_cols(sums[:o], -1) + sums[o:2 * o] + shift_cols(sums[2 * o:], 1)

    def add_row(q):
        for a in range(3):
            add_tap(first + q, a, q - a + 1)

    def sum_copy(r):
        return pltpu.make_async_remote_copy(
            src_ref=part.at[r + 1], dst_ref=peer.at[r], send_sem=sum_send.at[r], recv_sem=sum_recv.at[r],
            device_id={"in": sibling}, device_id_type=MESH,
        )

    def out_copy(r):
        return pltpu.make_async_remote_copy(
            src_ref=act.at[r, :, pl.ds(pl.multiple_of(c * half_c, half_c), half_c)],
            dst_ref=out.at[pl.ds(pl.multiple_of(p * o, o), o), :],
            send_sem=out_send.at[r], recv_sem=out_recv.at[p],
            device_id={"filt": r}, device_id_type=MESH,
        )

    own_out = pltpu.make_async_copy(
        act.at[p, :, pl.ds(pl.multiple_of(c * half_c, half_c), half_c)],
        out.at[pl.ds(pl.multiple_of(p * o, o), o), :],
        load_sem.at[0],
    )

    def g_copy(q, d):
        place = grads.at[1, :, lanes(q, cols)]
        return pltpu.make_async_remote_copy(
            src_ref=place, dst_ref=place, send_sem=g_send.at[d, q], recv_sem=g_recv.at[q],
            device_id={"sp": x_peers[d]}, device_id_type=MESH,
        )

    def done_at(r):
        low = jnp.where(s == 0, jnp.maximum(p, 1), jnp.maximum(p, n_f - p))
        high = jnp.where(
            s == n_s - 1, jnp.maximum(last - p, 1), jnp.maximum(last - p, p + 1)
        )
        return jnp.where(r == 0, low, jnp.where(r == last, high, jnp.abs(r - p) + 1))

    def finish(r):
        sum_copy(r).wait_recv()
        bias_all = jnp.broadcast_to(bias[...], (cols, o)).T
        shifted = part[r + 1] + peer[r] + bias_all
        sig = jax.nn.sigmoid(shifted)
        slope = sig * (1.0 + shifted * (1.0 - sig))
        grad = (cot[r].astype(jnp.float32) * slope).astype(jnp.bfloat16)
        place = lanes(first + r, cols)
        grads[1, :, place] = grad
        act[r] = (shifted * sig).astype(jnp.bfloat16)
        for d in range(n_s - 1):
            g_copy(first + r, d).start()

        @pl.when(r == p)
        def _():
            own_out.start()

        @pl.when(r != p)
        def _():
            out_copy(r).start()

        store_shifts(grads, place, grad)

    add_row(p)
    load_cot.wait()
    load_bias.wait()

    def relay(t):
        @pl.when(t == p + 1)
        def _():
            for block in x_peers:
                for h in range(2):
                    wait_row(block * n_f, h)

                    @pl.when(p < last)
                    def _():
                        to_right(block * n_f, h).start()

        @pl.when(t == n_f - p)
        def _():
            for block in x_peers:
                for h in range(2):
                    wait_row(block * n_f + last, h)

                    @pl.when(p > 0)
                    def _():
                        to_left(block * n_f + last, h).start()

    def add_edges(t):
        @pl.when((t == p + 1) & (s < n_s - 1))
        def _():
            add_tap(first + n_f, 2, last)

        @pl.when((t == n_f - p) & (s > 0))
        def _():
            add_tap(first - 1, 0, 0)

    def start_sums(t):
        @pl.loop(0, n_f)
        def _(r):
            @pl.when(done_at(r) == t)
            def _():
                sum_copy(r).start()

    def finish_rows(t):
        @pl.loop(0, n_f)
        def _(r):
            @pl.when(done_at(r) == t)
            def _():
                finish(r)

    @pl.loop(1, n_f)
    def _(t):
        for h in range(2):
            @pl.when(p - t >= 0)
            def _():
                wait_row(first + p - t, h)
                pass_on(p - t, h, True, False)

            @pl.when(p + t < n_f)
            def _():
                wait_row(first + p + t, h)
                pass_on(p + t, h, False, True)

        relay(t)

        @pl.when(p - t >= 0)
        def _():
            add_row(p - t)

        @pl.when(p + t < n_f)
        def _():
            add_row(p + t)

        add_edges(t)
        start_sums(t)
        finish_rows(t - 1)

    def own_rows():
        @pl.loop(0, 9)
        def _(k):
            gw_own[k] = rows_tap(rows, grads, k // 3, lax.rem(k, 3), early_row(s, n_f), n_f - 1)

    finish_rows(n_f - 1)
    if n_s <= 2:
        own_rows()
    relay(n_f)
    add_edges(n_f)
    start_sums(n_f)
    finish_rows(n_f)
    if n_s > 2:
        own_rows()

    def take_grad(q):
        g_copy(q, 0).wait_recv()
        place = lanes(q, cols)
        store_shifts(grads, place, grads[1, :, place])

    for block in x_peers:
        start = early_row(block, n_f)

        @pl.loop(1, last)
        def _(q):
            for h in range(2):
                wait_row(block * n_f + q, h)

        @pl.loop(0, n_f - 1)
        def _(q):
            take_grad(start + q)

        @pl.loop(0, 9)
        def _(k):
            gw_own[k] += rows_tap(rows, grads, k // 3, lax.rem(k, 3), start, n_f - 1)

    for block in x_peers:
        take_grad(late_row(block, n_f))

    @pl.loop(0, n_f)
    def _(r):
        sum_copy(r).wait_send()

        @pl.when(r == p)
        def _():
            own_out.wait()

        @pl.when(r != p)
        def _():
            out_copy(r).wait_send()
            pltpu.make_async_remote_copy(
                src_ref=act.at[r, :, pl.ds(0, half_c)],
                dst_ref=out.at[pl.ds(pl.multiple_of(r * o, o), o), :],
                send_sem=out_send.at[r], recv_sem=out_recv.at[r],
                device_id={"filt": r}, device_id_type=MESH,
            ).wait_recv()

        for d in range(n_s - 1):
            g_copy(first + r, d).wait_send()

            @pl.when(crosses(r))
            def _():
                for h in range(2):
                    to_x(r, h, d).wait_send()

        @pl.when((r <= p) & (p < last))
        def _():
            for h in range(2):
                to_right(first + r, h).wait_send()

        @pl.when((r >= p) & (p > 0))
        def _():
            for h in range(2):
                to_left(first + r, h).wait_send()

    for block in x_peers:
        for h in range(2):
            @pl.when(p < last)
            def _():
                to_right(block * n_f, h).wait_send()

            @pl.when(p > 0)
            def _():
                to_left(block * n_f + last, h).wait_send()


def finish_kernel(n_f, n_s, rows, grads, gw_own, out_in, gw, gb, out, total, sem, out_sem):
    out_copy = pltpu.make_async_copy(out_in, out.at[0], out_sem)
    out_copy.start()

    def gw_copy(k):
        return pltpu.make_async_copy(total.at[k], gw.at[k // 3, lax.rem(k, 3)], sem.at[k])

    @pl.loop(0, 9)
    def _(k):
        value = gw_own[k]
        for block in range(n_s):
            value = value + rows_tap(rows, grads, k // 3, lax.rem(k, 3), late_row(block, n_f), 1)
        total[k] = value
        gw_copy(k).start()

    gb[...] = lax.dot_general(
        jnp.ones((8, grads.shape[2]), jnp.bfloat16), grads[1], NT, preferred_element_type=jnp.float32
    )[:1]

    @pl.loop(0, 9)
    def _(k):
        gw_copy(k).wait()

    out_copy.wait()


def on_device(image, weight, bias, cotangent):
    n_f, n_s, n_in = (lax.axis_size(name) for name in ("filt", "sp", "in"))
    row_count, o, cols = cotangent.shape
    depth = image.shape[2]
    total = n_f * n_s
    any_space = pl.BlockSpec(memory_space=pl.ANY)
    vmem = pl.BlockSpec(memory_space=pltpu.VMEM)
    hbm = pl.BlockSpec(memory_space=pltpu.HBM)
    dma = pltpu.SemaphoreType.DMA
    between = pl.pallas_call(
        functools.partial(gather_kernel, n_f, n_s),
        out_shape=(
            pltpu.VMEM((total + 2, cols, depth), jnp.bfloat16),
            pltpu.VMEM((3, o, total * cols), jnp.bfloat16),
            pltpu.VMEM((9, o, depth), jnp.float32),
            pltpu.VMEM((n_f * o, cols // n_in), jnp.bfloat16),
        ),
        in_specs=[hbm, hbm, hbm, hbm],
        out_specs=(vmem,) * 4,
        scratch_shapes=[
            pltpu.VMEM((3, 3, o, depth), jnp.bfloat16),
            pltpu.VMEM((1, o), jnp.float32),
            pltpu.VMEM((n_f, o, cols), jnp.bfloat16),
            pltpu.VMEM((n_f + 2, o, cols), jnp.float32),
            pltpu.VMEM((n_f, o, cols), jnp.float32),
            pltpu.VMEM((n_f, o, cols), jnp.bfloat16),
            dma((4,)),
            dma((2, total, 2)),
            dma((total, 2)),
            dma((n_s - 1, n_f, 2)),
            dma((n_f,)),
            dma((n_f,)),
            dma((n_s - 1, total)),
            dma((total,)),
            dma((n_f,)),
            dma((n_f,)),
        ],
        compiler_params=pltpu.CompilerParams(
            collective_id=0, has_side_effects=True, vmem_limit_bytes=24 * 1024 * 1024
        ),
        name="gather",
    )(*(
        pltpu.with_memory_space_constraint(x, pltpu.HBM)
        for x in (image, weight, bias.reshape(1, o), cotangent)
    ))
    grad_weight, grad_bias, output = pl.pallas_call(
        functools.partial(finish_kernel, n_f, n_s),
        out_shape=(
            jax.ShapeDtypeStruct((3, 3, o, depth), jnp.float32),
            jax.ShapeDtypeStruct((1, o), jnp.float32),
            jax.ShapeDtypeStruct((1, n_f * o, cols // n_in), jnp.bfloat16),
        ),
        in_specs=[vmem] * 4,
        out_specs=(any_space, vmem, any_space),
        scratch_shapes=[
            pltpu.VMEM((9, o, depth), jnp.float32),
            dma((9,)),
            dma(()),
        ],
        compiler_params=pltpu.CompilerParams(vmem_limit_bytes=20 * 1024 * 1024),
        name="finish",
    )(*between)
    return (output, grad_weight, grad_bias.reshape(o))


def solution(mesh):
    placed = (
        P(("groups", "sp", "filt"), None, "in"),
        P(None, None, "filt", None),
        P("filt"),
        P(("groups", "sp"), "filt", None),
    )
    return jax.shard_map(
        on_device,
        mesh=mesh,
        in_specs=placed,
        out_specs=(
            P(("groups", "sp", "filt"), None, "in"),
            P("groups", None, "filt", "in"),
            P(("groups", "filt")),
        ),
        check_vma=False,
    )
```

```python
import functools

import jax
import jax.numpy as jnp
from jax import lax
from jax.experimental import pallas as pl
from jax.experimental.pallas import tpu as pltpu
from jax.sharding import PartitionSpec as P

MESH = pl.DeviceIdType.MESH
NT = (((1,), (1,)), ((), ()))


def shift_cols(value, by):
    cols = value.shape[1]
    col = lax.broadcasted_iota(jnp.int32, value.shape, 1)
    if by < 0:
        return jnp.where(col == 0, 0.0, pltpu.roll(value, 1, 1))
    return jnp.where(col == cols - 1, 0.0, pltpu.roll(value, cols - 1, 1))


def lanes(q, cols, count=1):
    return pl.ds(pl.multiple_of(q * cols, cols), count * cols)


def store_shifts(grads, place, grad):
    wide = grad.astype(jnp.float32)
    grads[0, :, place] = shift_cols(wide, 1).astype(jnp.bfloat16)
    grads[2, :, place] = shift_cols(wide, -1).astype(jnp.bfloat16)


def rows_tap(rows, grads, a, b, start, count):
    cols, depth = rows.shape[1], rows.shape[2]
    window = rows[pl.ds(start + a, count)].reshape(count * cols, depth)
    return jnp.dot(
        grads[b, :, lanes(start, cols, count)], window, preferred_element_type=jnp.float32
    )


def late_row(block, n_f):
    return block * n_f + jnp.where(block > 0, 0, n_f - 1)


def early_row(block, n_f):
    return block * n_f + jnp.where(block > 0, 1, 0)


def gather_kernel(
    n_f, n_s,
    image, weight, bias_in, cotangent,
    rows, grads, gw_own, out,
    w, bias, cot, part, peer, act,
    load_sem, row_send, row_recv, x_send, sum_send, sum_recv,
    g_send, g_recv, out_send, out_recv,
):
    p, s, c = lax.axis_index("filt"), lax.axis_index("sp"), lax.axis_index("in")
    sibling = 1 - c
    cols, depth = rows.shape[1], rows.shape[2]
    o = w.shape[2]
    half_c = out.shape[1]
    total = n_f * n_s
    first = s * n_f
    last = n_f - 1
    x_peers = [lax.rem(s + d, n_s) for d in range(1, n_s)]

    load_row = pltpu.make_async_copy(image.at[0], rows.at[1 + first + p], load_sem.at[0])
    load_w = pltpu.make_async_copy(
        weight.at[:, :, :, pl.ds(pl.multiple_of(c * depth, depth), depth)], w, load_sem.at[1]
    )
    load_cot = pltpu.make_async_copy(cotangent, cot, load_sem.at[2])
    load_bias = pltpu.make_async_copy(bias_in, bias, load_sem.at[3])
    load_row.start()
    load_w.start()
    load_cot.start()
    load_bias.start()

    barrier = pltpu.get_barrier_semaphore()
    for d in range(1, n_f):
        pl.semaphore_signal(barrier, 1, device_id={"filt": lax.rem(p + d, n_f)}, device_id_type=MESH)
    for peer_s in x_peers:
        pl.semaphore_signal(barrier, 1, device_id={"sp": peer_s}, device_id_type=MESH)
    pl.semaphore_signal(barrier, 1, device_id={"in": sibling}, device_id_type=MESH)
    pl.semaphore_wait(barrier, n_f - 1 + n_s - 1 + 1)

    piece = cols // 2

    def row_copy(q, h, way, where, send):
        slot = rows.at[1 + q, pl.ds(h * piece, piece)]
        return pltpu.make_async_remote_copy(
            src_ref=slot, dst_ref=slot, send_sem=send, recv_sem=row_recv.at[q, h],
            device_id={way: where}, device_id_type=MESH,
        )

    def to_right(q, h):
        return row_copy(q, h, "filt", p + 1, row_send.at[0, q, h])

    def to_left(q, h):
        return row_copy(q, h, "filt", p - 1, row_send.at[1, q, h])

    def to_x(q, h, d):
        return row_copy(first + q, h, "sp", x_peers[d], x_send.at[d, q, h])

    def wait_row(q, h):
        row_copy(q, h, "filt", p, row_send.at[0, 0, 0]).wait_recv()

    def crosses(q):
        return ((q > 0) & (q < last)) | (q == p)

    def pass_on(q, h, right, left):
        if right:
            @pl.when(p < last)
            def _():
                to_right(first + q, h).start()
        if left:
            @pl.when(p > 0)
            def _():
                to_left(first + q, h).start()

        @pl.when(crosses(q))
        def _():
            for d in range(n_s - 1):
                to_x(q, h, d).start()

    load_row.wait()
    for h in range(2):
        pass_on(p, h, True, True)

    zero = jnp.zeros((cols, depth), rows.dtype)
    rows[0] = zero
    rows[total + 1] = zero

    @pl.loop(0, n_f + 2)
    def _(r):
        part[r] = jnp.zeros((o, cols), jnp.float32)

    load_w.wait()

    def add_tap(q, a, r):
        sums = lax.dot_general(
            w[a].reshape(3 * o, depth), rows[1 + q], NT, preferred_element_type=jnp.float32
        )
        part[r + 1] += shift_cols(sums[:o], -1) + sums[o:2 * o] + shift_cols(sums[2 * o:], 1)

    def add_row(q):
        for a in range(3):
            add_tap(first + q, a, q - a + 1)

    def sum_copy(r):
        return pltpu.make_async_remote_copy(
            src_ref=part.at[r + 1], dst_ref=peer.at[r], send_sem=sum_send.at[r], recv_sem=sum_recv.at[r],
            device_id={"in": sibling}, device_id_type=MESH,
        )

    def out_copy(r):
        return pltpu.make_async_remote_copy(
            src_ref=act.at[r, :, pl.ds(pl.multiple_of(c * half_c, half_c), half_c)],
            dst_ref=out.at[pl.ds(pl.multiple_of(p * o, o), o), :],
            send_sem=out_send.at[r], recv_sem=out_recv.at[p],
            device_id={"filt": r}, device_id_type=MESH,
        )

    own_out = pltpu.make_async_copy(
        act.at[p, :, pl.ds(pl.multiple_of(c * half_c, half_c), half_c)],
        out.at[pl.ds(pl.multiple_of(p * o, o), o), :],
        load_sem.at[0],
    )

    def g_copy(q, d):
        place = grads.at[1, :, lanes(q, cols)]
        return pltpu.make_async_remote_copy(
            src_ref=place, dst_ref=place, send_sem=g_send.at[d, q], recv_sem=g_recv.at[q],
            device_id={"sp": x_peers[d]}, device_id_type=MESH,
        )

    def done_at(r):
        low = jnp.where(s == 0, jnp.maximum(p, 1), jnp.maximum(p, n_f - p))
        high = jnp.where(
            s == n_s - 1, jnp.maximum(last - p, 1), jnp.maximum(last - p, p + 1)
        )
        return jnp.where(r == 0, low, jnp.where(r == last, high, jnp.abs(r - p) + 1))

    def finish(r):
        sum_copy(r).wait_recv()
        bias_all = jnp.broadcast_to(bias[...], (cols, o)).T
        shifted = part[r + 1] + peer[r] + bias_all
        sig = jax.nn.sigmoid(shifted)
        slope = sig * (1.0 + shifted * (1.0 - sig))
        grad = (cot[r].astype(jnp.float32) * slope).astype(jnp.bfloat16)
        place = lanes(first + r, cols)
        grads[1, :, place] = grad
        act[r] = (shifted * sig).astype(jnp.bfloat16)
        for d in range(n_s - 1):
            g_copy(first + r, d).start()

        store_shifts(grads, place, grad)

    def send_out(r):
        @pl.when(r == p)
        def _():
            own_out.start()

        @pl.when(r != p)
        def _():
            out_copy(r).start()

    add_row(p)
    load_cot.wait()
    load_bias.wait()

    def relay(t):
        @pl.when(t == p + 1)
        def _():
            for block in x_peers:
                for h in range(2):
                    wait_row(block * n_f, h)

                    @pl.when(p < last)
                    def _():
                        to_right(block * n_f, h).start()

        @pl.when(t == n_f - p)
        def _():
            for block in x_peers:
                for h in range(2):
                    wait_row(block * n_f + last, h)

                    @pl.when(p > 0)
                    def _():
                        to_left(block * n_f + last, h).start()

    def add_edges(t):
        @pl.when((t == p + 1) & (s < n_s - 1))
        def _():
            add_tap(first + n_f, 2, last)

        @pl.when((t == n_f - p) & (s > 0))
        def _():
            add_tap(first - 1, 0, 0)

    def start_sums(t):
        @pl.loop(0, n_f)
        def _(r):
            @pl.when(done_at(r) == t)
            def _():
                sum_copy(r).start()

    def finish_rows(t):
        @pl.loop(0, n_f)
        def _(r):
            @pl.when(done_at(r) == t)
            def _():
                finish(r)

    @pl.loop(1, n_f)
    def _(t):
        for h in range(2):
            @pl.when(p - t >= 0)
            def _():
                wait_row(first + p - t, h)
                pass_on(p - t, h, True, False)

            @pl.when(p + t < n_f)
            def _():
                wait_row(first + p + t, h)
                pass_on(p + t, h, False, True)

        relay(t)

        @pl.when(p - t >= 0)
        def _():
            add_row(p - t)

        @pl.when(p + t < n_f)
        def _():
            add_row(p + t)

        add_edges(t)
        start_sums(t)
        finish_rows(t - 1)

    def own_rows():
        @pl.loop(0, 9)
        def _(k):
            gw_own[k] = rows_tap(rows, grads, k // 3, lax.rem(k, 3), early_row(s, n_f), n_f - 1)

    finish_rows(n_f - 1)
    if n_s <= 2:
        own_rows()
    relay(n_f)
    add_edges(n_f)
    start_sums(n_f)

    @pl.loop(0, n_f)
    def _(r):
        @pl.when(done_at(r) < n_f)
        def _():
            send_out(r)

    finish_rows(n_f)

    @pl.loop(0, n_f)
    def _(r):
        @pl.when(done_at(r) == n_f)
        def _():
            send_out(r)

    if n_s > 2:
        own_rows()

    def take_grad(q):
        g_copy(q, 0).wait_recv()
        place = lanes(q, cols)
        store_shifts(grads, place, grads[1, :, place])

    for block in x_peers:
        start = early_row(block, n_f)

        @pl.loop(1, last)
        def _(q):
            for h in range(2):
                wait_row(block * n_f + q, h)

        @pl.loop(0, n_f - 1)
        def _(q):
            take_grad(start + q)

        @pl.loop(0, 9)
        def _(k):
            gw_own[k] += rows_tap(rows, grads, k // 3, lax.rem(k, 3), start, n_f - 1)

    for block in x_peers:
        take_grad(late_row(block, n_f))

    @pl.loop(0, n_f)
    def _(r):
        sum_copy(r).wait_send()

        @pl.when(r == p)
        def _():
            own_out.wait()

        @pl.when(r != p)
        def _():
            out_copy(r).wait_send()
            pltpu.make_async_remote_copy(
                src_ref=act.at[r, :, pl.ds(0, half_c)],
                dst_ref=out.at[pl.ds(pl.multiple_of(r * o, o), o), :],
                send_sem=out_send.at[r], recv_sem=out_recv.at[r],
                device_id={"filt": r}, device_id_type=MESH,
            ).wait_recv()

        for d in range(n_s - 1):
            g_copy(first + r, d).wait_send()

            @pl.when(crosses(r))
            def _():
                for h in range(2):
                    to_x(r, h, d).wait_send()

        @pl.when((r <= p) & (p < last))
        def _():
            for h in range(2):
                to_right(first + r, h).wait_send()

        @pl.when((r >= p) & (p > 0))
        def _():
            for h in range(2):
                to_left(first + r, h).wait_send()

    for block in x_peers:
        for h in range(2):
            @pl.when(p < last)
            def _():
                to_right(block * n_f, h).wait_send()

            @pl.when(p > 0)
            def _():
                to_left(block * n_f + last, h).wait_send()


def finish_kernel(n_f, n_s, rows, grads, gw_own, out_in, gw, gb, out, total, sem, out_sem):
    out_copy = pltpu.make_async_copy(out_in, out.at[0], out_sem)
    out_copy.start()

    late = [(n_f - 1, min(n_s, 2))] + [(block * n_f, 1) for block in range(2, n_s)]

    def gw_copy(k):
        return pltpu.make_async_copy(total.at[k], gw.at[k // 3, lax.rem(k, 3)], sem.at[k])

    @pl.loop(0, 9)
    def _(k):
        value = gw_own[k]
        for start, count in late:
            value = value + rows_tap(rows, grads, k // 3, lax.rem(k, 3), start, count)
        total[k] = value
        gw_copy(k).start()

    gb[...] = lax.dot_general(
        jnp.ones((8, grads.shape[2]), jnp.bfloat16), grads[1], NT, preferred_element_type=jnp.float32
    )[:1]

    @pl.loop(0, 9)
    def _(k):
        gw_copy(k).wait()

    out_copy.wait()


def on_device(image, weight, bias, cotangent):
    n_f, n_s, n_in = (lax.axis_size(name) for name in ("filt", "sp", "in"))
    row_count, o, cols = cotangent.shape
    depth = image.shape[2]
    total = n_f * n_s
    any_space = pl.BlockSpec(memory_space=pl.ANY)
    vmem = pl.BlockSpec(memory_space=pltpu.VMEM)
    hbm = pl.BlockSpec(memory_space=pltpu.HBM)
    dma = pltpu.SemaphoreType.DMA
    between = pl.pallas_call(
        functools.partial(gather_kernel, n_f, n_s),
        out_shape=(
            pltpu.VMEM((total + 2, cols, depth), jnp.bfloat16),
            pltpu.VMEM((3, o, total * cols), jnp.bfloat16),
            pltpu.VMEM((9, o, depth), jnp.float32),
            pltpu.VMEM((n_f * o, cols // n_in), jnp.bfloat16),
        ),
        in_specs=[hbm, hbm, hbm, hbm],
        out_specs=(vmem,) * 4,
        scratch_shapes=[
            pltpu.VMEM((3, 3, o, depth), jnp.bfloat16),
            pltpu.VMEM((1, o), jnp.float32),
            pltpu.VMEM((n_f, o, cols), jnp.bfloat16),
            pltpu.VMEM((n_f + 2, o, cols), jnp.float32),
            pltpu.VMEM((n_f, o, cols), jnp.float32),
            pltpu.VMEM((n_f, o, cols), jnp.bfloat16),
            dma((4,)),
            dma((2, total, 2)),
            dma((total, 2)),
            dma((n_s - 1, n_f, 2)),
            dma((n_f,)),
            dma((n_f,)),
            dma((n_s - 1, total)),
            dma((total,)),
            dma((n_f,)),
            dma((n_f,)),
        ],
        compiler_params=pltpu.CompilerParams(
            collective_id=0, has_side_effects=True, vmem_limit_bytes=24 * 1024 * 1024
        ),
        name="gather",
    )(*(
        pltpu.with_memory_space_constraint(x, pltpu.HBM)
        for x in (image, weight, bias.reshape(1, o), cotangent)
    ))
    grad_weight, grad_bias, output = pl.pallas_call(
        functools.partial(finish_kernel, n_f, n_s),
        out_shape=(
            jax.ShapeDtypeStruct((3, 3, o, depth), jnp.float32),
            jax.ShapeDtypeStruct((1, o), jnp.float32),
            jax.ShapeDtypeStruct((1, n_f * o, cols // n_in), jnp.bfloat16),
        ),
        in_specs=[vmem] * 4,
        out_specs=(any_space, vmem, any_space),
        scratch_shapes=[
            pltpu.VMEM((9, o, depth), jnp.float32),
            dma((9,)),
            dma(()),
        ],
        compiler_params=pltpu.CompilerParams(vmem_limit_bytes=20 * 1024 * 1024),
        name="finish",
    )(*between)
    return (output, grad_weight, grad_bias.reshape(o))


def solution(mesh):
    placed = (
        P(("groups", "sp", "filt"), None, "in"),
        P(None, None, "filt", None),
        P("filt"),
        P(("groups", "sp"), "filt", None),
    )
    return jax.shard_map(
        on_device,
        mesh=mesh,
        in_specs=placed,
        out_specs=(
            P(("groups", "sp", "filt"), None, "in"),
            P("groups", None, "filt", "in"),
            P(("groups", "filt")),
        ),
        check_vma=False,
    )
```

```python
import functools

import jax
import jax.numpy as jnp
from jax import lax
from jax.experimental import pallas as pl
from jax.experimental.pallas import tpu as pltpu
from jax.sharding import PartitionSpec as P

MESH = pl.DeviceIdType.MESH
NT = (((1,), (1,)), ((), ()))


def shift_cols(value, by):
    cols = value.shape[1]
    col = lax.broadcasted_iota(jnp.int32, value.shape, 1)
    if by < 0:
        return jnp.where(col == 0, 0.0, pltpu.roll(value, 1, 1))
    return jnp.where(col == cols - 1, 0.0, pltpu.roll(value, cols - 1, 1))


def lanes(q, cols, count=1):
    return pl.ds(pl.multiple_of(q * cols, cols), count * cols)


def store_shifts(grads, place, grad):
    wide = grad.astype(jnp.float32)
    grads[0, :, place] = shift_cols(wide, 1).astype(jnp.bfloat16)
    grads[2, :, place] = shift_cols(wide, -1).astype(jnp.bfloat16)


def rows_tap(rows, grads, a, b, start, count):
    cols, depth = rows.shape[1], rows.shape[2]
    window = rows[pl.ds(start + a, count)].reshape(count * cols, depth)
    return jnp.dot(
        grads[b, :, lanes(start, cols, count)], window, preferred_element_type=jnp.float32
    )


def late_row(block, n_f):
    return block * n_f + jnp.where(block > 0, 0, n_f - 1)


def early_row(block, n_f):
    return block * n_f + jnp.where(block > 0, 1, 0)


def gather_kernel(
    n_f, n_s,
    image, weight, bias_in, cotangent,
    rows, grads, gw_own, out,
    w, bias, cot, part, peer, act,
    load_sem, row_send, row_recv, x_send, sum_send, sum_recv,
    g_send, g_recv, h_send, h_recv, out_send, out_recv,
):
    p, s, c = lax.axis_index("filt"), lax.axis_index("sp"), lax.axis_index("in")
    sibling = 1 - c
    cols, depth = rows.shape[1], rows.shape[2]
    o = w.shape[2]
    half_c = out.shape[1]
    total = n_f * n_s
    first = s * n_f
    last = n_f - 1
    x_peers = [lax.rem(s + d, n_s) for d in range(1, n_s)]

    load_row = pltpu.make_async_copy(image.at[0], rows.at[1 + first + p], load_sem.at[0])
    load_w = pltpu.make_async_copy(
        weight.at[:, :, :, pl.ds(pl.multiple_of(c * depth, depth), depth)], w, load_sem.at[1]
    )
    load_cot = pltpu.make_async_copy(cotangent, cot, load_sem.at[2])
    load_bias = pltpu.make_async_copy(bias_in, bias, load_sem.at[3])
    load_row.start()
    load_w.start()
    load_cot.start()
    load_bias.start()

    barrier = pltpu.get_barrier_semaphore()
    for d in range(1, n_f):
        pl.semaphore_signal(barrier, 1, device_id={"filt": lax.rem(p + d, n_f)}, device_id_type=MESH)
    for peer_s in x_peers:
        pl.semaphore_signal(barrier, 1, device_id={"sp": peer_s}, device_id_type=MESH)
    pl.semaphore_signal(barrier, 1, device_id={"in": sibling}, device_id_type=MESH)
    pl.semaphore_wait(barrier, n_f - 1 + n_s - 1 + 1)

    piece = cols // 2

    def row_copy(q, h, way, where, send):
        slot = rows.at[1 + q, pl.ds(h * piece, piece)]
        return pltpu.make_async_remote_copy(
            src_ref=slot, dst_ref=slot, send_sem=send, recv_sem=row_recv.at[q, h],
            device_id={way: where}, device_id_type=MESH,
        )

    def to_right(q, h):
        return row_copy(q, h, "filt", p + 1, row_send.at[0, q, h])

    def to_left(q, h):
        return row_copy(q, h, "filt", p - 1, row_send.at[1, q, h])

    def to_x(q, h, d):
        return row_copy(first + q, h, "sp", x_peers[d], x_send.at[d, q, h])

    def wait_row(q, h):
        row_copy(q, h, "filt", p, row_send.at[0, 0, 0]).wait_recv()

    def crosses(q):
        return ((q > 0) & (q < last)) | (q == p)

    def pass_on(q, h, right, left):
        if right:
            @pl.when(p < last)
            def _():
                to_right(first + q, h).start()
        if left:
            @pl.when(p > 0)
            def _():
                to_left(first + q, h).start()

        @pl.when(crosses(q))
        def _():
            for d in range(n_s - 1):
                to_x(q, h, d).start()

    load_row.wait()
    for h in range(2):
        pass_on(p, h, True, True)

    zero = jnp.zeros((cols, depth), rows.dtype)
    rows[0] = zero
    rows[total + 1] = zero

    @pl.loop(0, n_f + 2)
    def _(r):
        part[r] = jnp.zeros((o, cols), jnp.float32)

    load_w.wait()

    def add_tap(q, a, r):
        sums = lax.dot_general(
            w[a].reshape(3 * o, depth), rows[1 + q], NT, preferred_element_type=jnp.float32
        )
        part[r + 1] += shift_cols(sums[:o], -1) + sums[o:2 * o] + shift_cols(sums[2 * o:], 1)

    def add_row(q):
        for a in range(3):
            add_tap(first + q, a, q - a + 1)

    def sum_copy(r):
        return pltpu.make_async_remote_copy(
            src_ref=part.at[r + 1], dst_ref=peer.at[r], send_sem=sum_send.at[r], recv_sem=sum_recv.at[r],
            device_id={"in": sibling}, device_id_type=MESH,
        )

    def out_copy(r):
        return pltpu.make_async_remote_copy(
            src_ref=act.at[r, :, pl.ds(pl.multiple_of(c * half_c, half_c), half_c)],
            dst_ref=out.at[pl.ds(pl.multiple_of(p * o, o), o), :],
            send_sem=out_send.at[r], recv_sem=out_recv.at[p],
            device_id={"filt": r}, device_id_type=MESH,
        )

    own_out = pltpu.make_async_copy(
        act.at[p, :, pl.ds(pl.multiple_of(c * half_c, half_c), half_c)],
        out.at[pl.ds(pl.multiple_of(p * o, o), o), :],
        load_sem.at[0],
    )

    half_o = o // 2

    def g_half(q, core):
        return grads.at[1, pl.ds(pl.multiple_of(core * half_o, half_o), half_o), lanes(q, cols)]

    def g_copy(q, d):
        place = g_half(q, c)
        return pltpu.make_async_remote_copy(
            src_ref=place, dst_ref=place, send_sem=g_send.at[d, q], recv_sem=g_recv.at[q],
            device_id={"sp": x_peers[d]}, device_id_type=MESH,
        )

    def h_copy(q, core):
        place = g_half(q, core)
        return pltpu.make_async_remote_copy(
            src_ref=place, dst_ref=place, send_sem=h_send.at[q], recv_sem=h_recv.at[q],
            device_id={"in": sibling}, device_id_type=MESH,
        )

    def done_at(r):
        low = jnp.where(s == 0, jnp.maximum(p, 1), jnp.maximum(p, n_f - p))
        high = jnp.where(
            s == n_s - 1, jnp.maximum(last - p, 1), jnp.maximum(last - p, p + 1)
        )
        return jnp.where(r == 0, low, jnp.where(r == last, high, jnp.abs(r - p) + 1))

    def finish(r):
        sum_copy(r).wait_recv()
        bias_all = jnp.broadcast_to(bias[...], (cols, o)).T
        shifted = part[r + 1] + peer[r] + bias_all
        sig = jax.nn.sigmoid(shifted)
        slope = sig * (1.0 + shifted * (1.0 - sig))
        grad = (cot[r].astype(jnp.float32) * slope).astype(jnp.bfloat16)
        place = lanes(first + r, cols)
        grads[1, :, place] = grad
        act[r] = (shifted * sig).astype(jnp.bfloat16)
        for d in range(n_s - 1):
            g_copy(first + r, d).start()

        store_shifts(grads, place, grad)

    def send_out(r):
        @pl.when(r == p)
        def _():
            own_out.start()

        @pl.when(r != p)
        def _():
            out_copy(r).start()

    add_row(p)
    load_cot.wait()
    load_bias.wait()

    def relay(t):
        @pl.when(t == p + 1)
        def _():
            for block in x_peers:
                for h in range(2):
                    wait_row(block * n_f, h)

                    @pl.when(p < last)
                    def _():
                        to_right(block * n_f, h).start()

        @pl.when(t == n_f - p)
        def _():
            for block in x_peers:
                for h in range(2):
                    wait_row(block * n_f + last, h)

                    @pl.when(p > 0)
                    def _():
                        to_left(block * n_f + last, h).start()

    def add_edges(t):
        @pl.when((t == p + 1) & (s < n_s - 1))
        def _():
            add_tap(first + n_f, 2, last)

        @pl.when((t == n_f - p) & (s > 0))
        def _():
            add_tap(first - 1, 0, 0)

    def start_sums(t):
        @pl.loop(0, n_f)
        def _(r):
            @pl.when(done_at(r) == t)
            def _():
                sum_copy(r).start()

    def finish_rows(t):
        @pl.loop(0, n_f)
        def _(r):
            @pl.when(done_at(r) == t)
            def _():
                finish(r)

    @pl.loop(1, n_f)
    def _(t):
        for h in range(2):
            @pl.when(p - t >= 0)
            def _():
                wait_row(first + p - t, h)
                pass_on(p - t, h, True, False)

            @pl.when(p + t < n_f)
            def _():
                wait_row(first + p + t, h)
                pass_on(p + t, h, False, True)

        relay(t)

        @pl.when(p - t >= 0)
        def _():
            add_row(p - t)

        @pl.when(p + t < n_f)
        def _():
            add_row(p + t)

        add_edges(t)
        start_sums(t)
        finish_rows(t - 1)

    def own_rows():
        @pl.loop(0, 9)
        def _(k):
            gw_own[k] = rows_tap(rows, grads, k // 3, lax.rem(k, 3), early_row(s, n_f), n_f - 1)

    finish_rows(n_f - 1)
    if n_s <= 2:
        own_rows()
    relay(n_f)
    add_edges(n_f)
    start_sums(n_f)

    @pl.loop(0, n_f)
    def _(r):
        @pl.when(done_at(r) < n_f)
        def _():
            send_out(r)

    finish_rows(n_f)

    @pl.loop(0, n_f)
    def _(r):
        @pl.when(done_at(r) == n_f)
        def _():
            send_out(r)

    if n_s > 2:
        own_rows()

    def share_grad(q):
        g_copy(q, 0).wait_recv()
        h_copy(q, c).start()

    def take_grad(q):
        h_copy(q, sibling).wait_recv()
        place = lanes(q, cols)
        store_shifts(grads, place, grads[1, :, place])

    for block in x_peers:
        start = early_row(block, n_f)

        @pl.loop(1, last)
        def _(q):
            for h in range(2):
                wait_row(block * n_f + q, h)

        @pl.loop(0, n_f - 1)
        def _(q):
            share_grad(start + q)

        @pl.loop(0, n_f - 1)
        def _(q):
            take_grad(start + q)

        @pl.loop(0, 9)
        def _(k):
            gw_own[k] += rows_tap(rows, grads, k // 3, lax.rem(k, 3), start, n_f - 1)

    for block in x_peers:
        share_grad(late_row(block, n_f))
        take_grad(late_row(block, n_f))

    @pl.loop(0, n_f)
    def _(r):
        sum_copy(r).wait_send()

        @pl.when(r == p)
        def _():
            own_out.wait()

        @pl.when(r != p)
        def _():
            out_copy(r).wait_send()
            pltpu.make_async_remote_copy(
                src_ref=act.at[r, :, pl.ds(0, half_c)],
                dst_ref=out.at[pl.ds(pl.multiple_of(r * o, o), o), :],
                send_sem=out_send.at[r], recv_sem=out_recv.at[r],
                device_id={"filt": r}, device_id_type=MESH,
            ).wait_recv()

        for d in range(n_s - 1):
            g_copy(first + r, d).wait_send()

            @pl.when(crosses(r))
            def _():
                for h in range(2):
                    to_x(r, h, d).wait_send()

        @pl.when((r <= p) & (p < last))
        def _():
            for h in range(2):
                to_right(first + r, h).wait_send()

        @pl.when((r >= p) & (p > 0))
        def _():
            for h in range(2):
                to_left(first + r, h).wait_send()

    for block in x_peers:
        @pl.loop(0, n_f)
        def _(q):
            h_copy(block * n_f + q, c).wait_send()

        for h in range(2):
            @pl.when(p < last)
            def _():
                to_right(block * n_f, h).wait_send()

            @pl.when(p > 0)
            def _():
                to_left(block * n_f + last, h).wait_send()


def finish_kernel(n_f, n_s, rows, grads, gw_own, out_in, gw, gb, out, total, sem, out_sem):
    out_copy = pltpu.make_async_copy(out_in, out.at[0], out_sem)
    out_copy.start()

    late = [(n_f - 1, min(n_s, 2))] + [(block * n_f, 1) for block in range(2, n_s)]

    def gw_copy(k):
        return pltpu.make_async_copy(total.at[k], gw.at[k // 3, lax.rem(k, 3)], sem.at[k])

    @pl.loop(0, 9)
    def _(k):
        value = gw_own[k]
        for start, count in late:
            value = value + rows_tap(rows, grads, k // 3, lax.rem(k, 3), start, count)
        total[k] = value
        gw_copy(k).start()

    gb[...] = lax.dot_general(
        jnp.ones((8, grads.shape[2]), jnp.bfloat16), grads[1], NT, preferred_element_type=jnp.float32
    )[:1]

    @pl.loop(0, 9)
    def _(k):
        gw_copy(k).wait()

    out_copy.wait()


def on_device(image, weight, bias, cotangent):
    n_f, n_s, n_in = (lax.axis_size(name) for name in ("filt", "sp", "in"))
    row_count, o, cols = cotangent.shape
    depth = image.shape[2]
    total = n_f * n_s
    any_space = pl.BlockSpec(memory_space=pl.ANY)
    vmem = pl.BlockSpec(memory_space=pltpu.VMEM)
    hbm = pl.BlockSpec(memory_space=pltpu.HBM)
    dma = pltpu.SemaphoreType.DMA
    between = pl.pallas_call(
        functools.partial(gather_kernel, n_f, n_s),
        out_shape=(
            pltpu.VMEM((total + 2, cols, depth), jnp.bfloat16),
            pltpu.VMEM((3, o, total * cols), jnp.bfloat16),
            pltpu.VMEM((9, o, depth), jnp.float32),
            pltpu.VMEM((n_f * o, cols // n_in), jnp.bfloat16),
        ),
        in_specs=[hbm, hbm, hbm, hbm],
        out_specs=(vmem,) * 4,
        scratch_shapes=[
            pltpu.VMEM((3, 3, o, depth), jnp.bfloat16),
            pltpu.VMEM((1, o), jnp.float32),
            pltpu.VMEM((n_f, o, cols), jnp.bfloat16),
            pltpu.VMEM((n_f + 2, o, cols), jnp.float32),
            pltpu.VMEM((n_f, o, cols), jnp.float32),
            pltpu.VMEM((n_f, o, cols), jnp.bfloat16),
            dma((4,)),
            dma((2, total, 2)),
            dma((total, 2)),
            dma((n_s - 1, n_f, 2)),
            dma((n_f,)),
            dma((n_f,)),
            dma((n_s - 1, total)),
            dma((total,)),
            dma((total,)),
            dma((total,)),
            dma((n_f,)),
            dma((n_f,)),
        ],
        compiler_params=pltpu.CompilerParams(
            collective_id=0, has_side_effects=True, vmem_limit_bytes=24 * 1024 * 1024
        ),
        name="gather",
    )(*(
        pltpu.with_memory_space_constraint(x, pltpu.HBM)
        for x in (image, weight, bias.reshape(1, o), cotangent)
    ))
    grad_weight, grad_bias, output = pl.pallas_call(
        functools.partial(finish_kernel, n_f, n_s),
        out_shape=(
            jax.ShapeDtypeStruct((3, 3, o, depth), jnp.float32),
            jax.ShapeDtypeStruct((1, o), jnp.float32),
            jax.ShapeDtypeStruct((1, n_f * o, cols // n_in), jnp.bfloat16),
        ),
        in_specs=[vmem] * 4,
        out_specs=(any_space, vmem, any_space),
        scratch_shapes=[
            pltpu.VMEM((9, o, depth), jnp.float32),
            dma((9,)),
            dma(()),
        ],
        compiler_params=pltpu.CompilerParams(vmem_limit_bytes=20 * 1024 * 1024),
        name="finish",
    )(*between)
    return (output, grad_weight, grad_bias.reshape(o))


def solution(mesh):
    placed = (
        P(("groups", "sp", "filt"), None, "in"),
        P(None, None, "filt", None),
        P("filt"),
        P(("groups", "sp"), "filt", None),
    )
    return jax.shard_map(
        on_device,
        mesh=mesh,
        in_specs=placed,
        out_specs=(
            P(("groups", "sp", "filt"), None, "in"),
            P("groups", None, "filt", "in"),
            P(("groups", "filt")),
        ),
        check_vma=False,
    )
```

```python
import functools

import jax
import jax.numpy as jnp
from jax import lax
from jax.experimental import pallas as pl
from jax.experimental.pallas import tpu as pltpu
from jax.sharding import PartitionSpec as P

MESH = pl.DeviceIdType.MESH
NT = (((1,), (1,)), ((), ()))


def shift_cols(value, by):
    cols = value.shape[1]
    col = lax.broadcasted_iota(jnp.int32, value.shape, 1)
    if by < 0:
        return jnp.where(col == 0, 0.0, pltpu.roll(value, 1, 1))
    return jnp.where(col == cols - 1, 0.0, pltpu.roll(value, cols - 1, 1))


def lanes(q, cols, count=1):
    return pl.ds(pl.multiple_of(q * cols, cols), count * cols)


def store_shifts(grads, place, grad):
    wide = grad.astype(jnp.float32)
    grads[0, :, place] = shift_cols(wide, 1).astype(jnp.bfloat16)
    grads[2, :, place] = shift_cols(wide, -1).astype(jnp.bfloat16)


def rows_tap(rows, grads, a, b, start, count):
    cols, depth = rows.shape[1], rows.shape[2]
    window = rows[pl.ds(start + a, count)].reshape(count * cols, depth)
    return jnp.dot(
        grads[b, :, lanes(start, cols, count)], window, preferred_element_type=jnp.float32
    )


def late_row(block, n_f):
    return block * n_f + jnp.where(block > 0, 0, n_f - 1)


def early_row(block, n_f):
    return block * n_f + jnp.where(block > 0, 1, 0)


def gather_kernel(
    n_f, n_s,
    image, weight, bias_in, cotangent,
    rows, grads, gw_own, out,
    w, bias, cot, part, peer, act,
    load_sem, row_send, row_recv, x_send, sum_send, sum_recv,
    g_send, g_recv, h_send, h_recv, out_send, out_recv,
):
    p, s, c = lax.axis_index("filt"), lax.axis_index("sp"), lax.axis_index("in")
    sibling = 1 - c
    cols, depth = rows.shape[1], rows.shape[2]
    o = w.shape[2]
    half_c = out.shape[1]
    total = n_f * n_s
    first = s * n_f
    last = n_f - 1
    x_peers = [lax.rem(s + d, n_s) for d in range(1, n_s)]

    load_row = pltpu.make_async_copy(image.at[0], rows.at[1 + first + p], load_sem.at[0])
    load_w = pltpu.make_async_copy(
        weight.at[:, :, :, pl.ds(pl.multiple_of(c * depth, depth), depth)], w, load_sem.at[1]
    )
    load_cot = pltpu.make_async_copy(cotangent, cot, load_sem.at[2])
    load_bias = pltpu.make_async_copy(bias_in, bias, load_sem.at[3])
    load_row.start()
    load_w.start()
    load_cot.start()
    load_bias.start()

    barrier = pltpu.get_barrier_semaphore()
    for d in range(1, n_f):
        pl.semaphore_signal(barrier, 1, device_id={"filt": lax.rem(p + d, n_f)}, device_id_type=MESH)
    for peer_s in x_peers:
        pl.semaphore_signal(barrier, 1, device_id={"sp": peer_s}, device_id_type=MESH)
    pl.semaphore_signal(barrier, 1, device_id={"in": sibling}, device_id_type=MESH)
    pl.semaphore_wait(barrier, n_f - 1 + n_s - 1 + 1)

    piece = cols // 2

    def row_copy(q, h, way, where, send):
        slot = rows.at[1 + q, pl.ds(h * piece, piece)]
        return pltpu.make_async_remote_copy(
            src_ref=slot, dst_ref=slot, send_sem=send, recv_sem=row_recv.at[q, h],
            device_id={way: where}, device_id_type=MESH,
        )

    def to_right(q, h):
        return row_copy(q, h, "filt", p + 1, row_send.at[0, q, h])

    def to_left(q, h):
        return row_copy(q, h, "filt", p - 1, row_send.at[1, q, h])

    def to_x(q, h, d):
        return row_copy(first + q, h, "sp", x_peers[d], x_send.at[d, q, h])

    def wait_row(q, h):
        row_copy(q, h, "filt", p, row_send.at[0, 0, 0]).wait_recv()

    def crosses(q, h):
        return ((q > 0) & (q < last)) | (q == p) | (h == 1)

    def pass_on(q, h, right, left):
        if right:
            @pl.when(p < last)
            def _():
                to_right(first + q, h).start()
        if left:
            @pl.when(p > 0)
            def _():
                to_left(first + q, h).start()

        @pl.when(crosses(q, h))
        def _():
            for d in range(n_s - 1):
                to_x(q, h, d).start()

    load_row.wait()
    for h in range(2):
        pass_on(p, h, True, True)

    zero = jnp.zeros((cols, depth), rows.dtype)
    rows[0] = zero
    rows[total + 1] = zero

    @pl.loop(0, n_f + 2)
    def _(r):
        part[r] = jnp.zeros((o, cols), jnp.float32)

    load_w.wait()

    def add_tap(q, a, r):
        sums = lax.dot_general(
            w[a].reshape(3 * o, depth), rows[1 + q], NT, preferred_element_type=jnp.float32
        )
        part[r + 1] += shift_cols(sums[:o], -1) + sums[o:2 * o] + shift_cols(sums[2 * o:], 1)

    def add_row(q):
        for a in range(3):
            add_tap(first + q, a, q - a + 1)

    def sum_copy(r):
        return pltpu.make_async_remote_copy(
            src_ref=part.at[r + 1], dst_ref=peer.at[r], send_sem=sum_send.at[r], recv_sem=sum_recv.at[r],
            device_id={"in": sibling}, device_id_type=MESH,
        )

    def out_copy(r):
        return pltpu.make_async_remote_copy(
            src_ref=act.at[r, :, pl.ds(pl.multiple_of(c * half_c, half_c), half_c)],
            dst_ref=out.at[pl.ds(pl.multiple_of(p * o, o), o), :],
            send_sem=out_send.at[r], recv_sem=out_recv.at[p],
            device_id={"filt": r}, device_id_type=MESH,
        )

    own_out = pltpu.make_async_copy(
        act.at[p, :, pl.ds(pl.multiple_of(c * half_c, half_c), half_c)],
        out.at[pl.ds(pl.multiple_of(p * o, o), o), :],
        load_sem.at[0],
    )

    half_o = o // 2

    def g_half(q, core):
        return grads.at[1, pl.ds(pl.multiple_of(core * half_o, half_o), half_o), lanes(q, cols)]

    def g_copy(q, d):
        place = g_half(q, c)
        return pltpu.make_async_remote_copy(
            src_ref=place, dst_ref=place, send_sem=g_send.at[d, q], recv_sem=g_recv.at[q],
            device_id={"sp": x_peers[d]}, device_id_type=MESH,
        )

    def h_copy(q, core):
        place = g_half(q, core)
        return pltpu.make_async_remote_copy(
            src_ref=place, dst_ref=place, send_sem=h_send.at[q], recv_sem=h_recv.at[q],
            device_id={"in": sibling}, device_id_type=MESH,
        )

    def done_at(r):
        low = jnp.where(s == 0, jnp.maximum(p, 1), jnp.maximum(p, n_f - p))
        high = jnp.where(
            s == n_s - 1, jnp.maximum(last - p, 1), jnp.maximum(last - p, p + 1)
        )
        return jnp.where(r == 0, low, jnp.where(r == last, high, jnp.abs(r - p) + 1))

    def finish(r):
        sum_copy(r).wait_recv()
        bias_all = jnp.broadcast_to(bias[...], (cols, o)).T
        shifted = part[r + 1] + peer[r] + bias_all
        sig = jax.nn.sigmoid(shifted)
        slope = sig * (1.0 + shifted * (1.0 - sig))
        grad = (cot[r].astype(jnp.float32) * slope).astype(jnp.bfloat16)
        place = lanes(first + r, cols)
        grads[1, :, place] = grad
        act[r] = (shifted * sig).astype(jnp.bfloat16)
        for d in range(n_s - 1):
            g_copy(first + r, d).start()

        store_shifts(grads, place, grad)

    def send_out(r):
        @pl.when(r == p)
        def _():
            own_out.start()

        @pl.when(r != p)
        def _():
            out_copy(r).start()

    add_row(p)
    load_cot.wait()
    load_bias.wait()

    def relay(t):
        @pl.when(t == p + 1)
        def _():
            for block in x_peers:
                wait_row(block * n_f, 0)

                @pl.when(p < last)
                def _():
                    to_right(block * n_f, 0).start()

                wait_row(block * n_f, 1)

        @pl.when(t == n_f - p)
        def _():
            for block in x_peers:
                wait_row(block * n_f + last, 0)

                @pl.when(p > 0)
                def _():
                    to_left(block * n_f + last, 0).start()

                wait_row(block * n_f + last, 1)

    def add_edges(t):
        @pl.when((t == p + 1) & (s < n_s - 1))
        def _():
            add_tap(first + n_f, 2, last)

        @pl.when((t == n_f - p) & (s > 0))
        def _():
            add_tap(first - 1, 0, 0)

    def start_sums(t):
        @pl.loop(0, n_f)
        def _(r):
            @pl.when(done_at(r) == t)
            def _():
                sum_copy(r).start()

    def finish_rows(t):
        @pl.loop(0, n_f)
        def _(r):
            @pl.when(done_at(r) == t)
            def _():
                finish(r)

    @pl.loop(1, n_f)
    def _(t):
        for h in range(2):
            @pl.when(p - t >= 0)
            def _():
                wait_row(first + p - t, h)
                pass_on(p - t, h, True, False)

            @pl.when(p + t < n_f)
            def _():
                wait_row(first + p + t, h)
                pass_on(p + t, h, False, True)

        relay(t)

        @pl.when(p - t >= 0)
        def _():
            add_row(p - t)

        @pl.when(p + t < n_f)
        def _():
            add_row(p + t)

        add_edges(t)
        start_sums(t)
        finish_rows(t - 1)

    def own_rows():
        @pl.loop(0, 9)
        def _(k):
            gw_own[k] = rows_tap(rows, grads, k // 3, lax.rem(k, 3), early_row(s, n_f), n_f - 1)

    finish_rows(n_f - 1)
    if n_s <= 2:
        own_rows()
    relay(n_f)
    add_edges(n_f)
    start_sums(n_f)

    @pl.loop(0, n_f)
    def _(r):
        @pl.when(done_at(r) < n_f)
        def _():
            send_out(r)

    finish_rows(n_f)

    @pl.loop(0, n_f)
    def _(r):
        @pl.when(done_at(r) == n_f)
        def _():
            send_out(r)

    if n_s > 2:
        own_rows()

    def share_grad(q):
        g_copy(q, 0).wait_recv()
        h_copy(q, c).start()

    def take_grad(q):
        h_copy(q, sibling).wait_recv()
        place = lanes(q, cols)
        store_shifts(grads, place, grads[1, :, place])

    for block in x_peers:
        start = early_row(block, n_f)

        @pl.loop(1, last)
        def _(q):
            for h in range(2):
                wait_row(block * n_f + q, h)

        @pl.loop(0, n_f - 1)
        def _(q):
            share_grad(start + q)

        @pl.loop(0, n_f - 1)
        def _(q):
            take_grad(start + q)

        @pl.loop(0, 9)
        def _(k):
            gw_own[k] += rows_tap(rows, grads, k // 3, lax.rem(k, 3), start, n_f - 1)

    for block in x_peers:
        share_grad(late_row(block, n_f))
        take_grad(late_row(block, n_f))

    @pl.loop(0, n_f)
    def _(r):
        sum_copy(r).wait_send()

        @pl.when(r == p)
        def _():
            own_out.wait()

        @pl.when(r != p)
        def _():
            out_copy(r).wait_send()
            pltpu.make_async_remote_copy(
                src_ref=act.at[r, :, pl.ds(0, half_c)],
                dst_ref=out.at[pl.ds(pl.multiple_of(r * o, o), o), :],
                send_sem=out_send.at[r], recv_sem=out_recv.at[r],
                device_id={"filt": r}, device_id_type=MESH,
            ).wait_recv()

        for d in range(n_s - 1):
            g_copy(first + r, d).wait_send()

            for h in range(2):
                @pl.when(crosses(r, h))
                def _():
                    to_x(r, h, d).wait_send()

        @pl.when((r <= p) & (p < last))
        def _():
            for h in range(2):
                to_right(first + r, h).wait_send()

        @pl.when((r >= p) & (p > 0))
        def _():
            for h in range(2):
                to_left(first + r, h).wait_send()

    for block in x_peers:
        @pl.loop(0, n_f)
        def _(q):
            h_copy(block * n_f + q, c).wait_send()

        @pl.when(p < last)
        def _():
            to_right(block * n_f, 0).wait_send()

        @pl.when(p > 0)
        def _():
            to_left(block * n_f + last, 0).wait_send()


def finish_kernel(n_f, n_s, rows, grads, gw_own, out_in, gw, gb, out, total, sem, out_sem):
    out_copy = pltpu.make_async_copy(out_in, out.at[0], out_sem)
    out_copy.start()

    late = [(n_f - 1, min(n_s, 2))] + [(block * n_f, 1) for block in range(2, n_s)]

    def gw_copy(k):
        return pltpu.make_async_copy(total.at[k], gw.at[k // 3, lax.rem(k, 3)], sem.at[k])

    @pl.loop(0, 9)
    def _(k):
        value = gw_own[k]
        for start, count in late:
            value = value + rows_tap(rows, grads, k // 3, lax.rem(k, 3), start, count)
        total[k] = value
        gw_copy(k).start()

    gb[...] = lax.dot_general(
        jnp.ones((8, grads.shape[2]), jnp.bfloat16), grads[1], NT, preferred_element_type=jnp.float32
    )[:1]

    @pl.loop(0, 9)
    def _(k):
        gw_copy(k).wait()

    out_copy.wait()


def on_device(image, weight, bias, cotangent):
    n_f, n_s, n_in = (lax.axis_size(name) for name in ("filt", "sp", "in"))
    row_count, o, cols = cotangent.shape
    depth = image.shape[2]
    total = n_f * n_s
    any_space = pl.BlockSpec(memory_space=pl.ANY)
    vmem = pl.BlockSpec(memory_space=pltpu.VMEM)
    hbm = pl.BlockSpec(memory_space=pltpu.HBM)
    dma = pltpu.SemaphoreType.DMA
    between = pl.pallas_call(
        functools.partial(gather_kernel, n_f, n_s),
        out_shape=(
            pltpu.VMEM((total + 2, cols, depth), jnp.bfloat16),
            pltpu.VMEM((3, o, total * cols), jnp.bfloat16),
            pltpu.VMEM((9, o, depth), jnp.float32),
            pltpu.VMEM((n_f * o, cols // n_in), jnp.bfloat16),
        ),
        in_specs=[hbm, hbm, hbm, hbm],
        out_specs=(vmem,) * 4,
        scratch_shapes=[
            pltpu.VMEM((3, 3, o, depth), jnp.bfloat16),
            pltpu.VMEM((1, o), jnp.float32),
            pltpu.VMEM((n_f, o, cols), jnp.bfloat16),
            pltpu.VMEM((n_f + 2, o, cols), jnp.float32),
            pltpu.VMEM((n_f, o, cols), jnp.float32),
            pltpu.VMEM((n_f, o, cols), jnp.bfloat16),
            dma((4,)),
            dma((2, total, 2)),
            dma((total, 2)),
            dma((n_s - 1, n_f, 2)),
            dma((n_f,)),
            dma((n_f,)),
            dma((n_s - 1, total)),
            dma((total,)),
            dma((total,)),
            dma((total,)),
            dma((n_f,)),
            dma((n_f,)),
        ],
        compiler_params=pltpu.CompilerParams(
            collective_id=0, has_side_effects=True, vmem_limit_bytes=24 * 1024 * 1024
        ),
        name="gather",
    )(*(
        pltpu.with_memory_space_constraint(x, pltpu.HBM)
        for x in (image, weight, bias.reshape(1, o), cotangent)
    ))
    grad_weight, grad_bias, output = pl.pallas_call(
        functools.partial(finish_kernel, n_f, n_s),
        out_shape=(
            jax.ShapeDtypeStruct((3, 3, o, depth), jnp.float32),
            jax.ShapeDtypeStruct((1, o), jnp.float32),
            jax.ShapeDtypeStruct((1, n_f * o, cols // n_in), jnp.bfloat16),
        ),
        in_specs=[vmem] * 4,
        out_specs=(any_space, vmem, any_space),
        scratch_shapes=[
            pltpu.VMEM((9, o, depth), jnp.float32),
            dma((9,)),
            dma(()),
        ],
        compiler_params=pltpu.CompilerParams(vmem_limit_bytes=20 * 1024 * 1024),
        name="finish",
    )(*between)
    return (output, grad_weight, grad_bias.reshape(o))


def solution(mesh):
    placed = (
        P(("groups", "sp", "filt"), None, "in"),
        P(None, None, "filt", None),
        P("filt"),
        P(("groups", "sp"), "filt", None),
    )
    return jax.shard_map(
        on_device,
        mesh=mesh,
        in_specs=placed,
        out_specs=(
            P(("groups", "sp", "filt"), None, "in"),
            P("groups", None, "filt", "in"),
            P(("groups", "filt")),
        ),
        check_vma=False,
    )
```
